512 devices in a mesh: snap: 8 (over y_hi, x), lat: 64 (over y_lo, z, core).
Axes of the slice: x: 4, y: 8 (y_hi: 2, y_lo: 4; y = y_hi * 4 + y_lo), z: 8, core: 2. Of those that a mesh axis runs over, the one named last changes fastest.
Arguments:
- activations: bfloat16 [8, 640, 1536], P('snap', 'lat'), may hold values from -6 to 6
- enc_weight: bfloat16 [8, 1536, 8192], P('snap', None, 'lat'), may hold values from -0.0546875 to 0.0546875
- enc_bias: float32 [8192], P('lat'), may hold values from -3 to 3
- dec_weight: bfloat16 [8192, 8, 1536], P('lat', 'snap'), may hold values from -0.125 to 0.125
- dec_bias: float32 [8, 1536], P('snap'), may hold values from -3 to 3
- dec_first: float32 [8192, 8, 1536], P('lat', 'snap'), may hold values from -0.3 to 0.3
- dec_second: float32 [8192, 8, 1536], P('lat', 'snap'), may hold values from 0.05 to 2
Outputs:
- enc_grad: bfloat16 [8, 1536, 8192], P('snap', None, 'lat')
- new_decoder: float32 [8192, 8, 1536], P('lat', 'snap')
- new_first: float32 [8192, 8, 1536], P('lat', 'snap')
- new_second: float32 [8192, 8, 1536], P('lat', 'snap')
The draws below stay inside these ranges and needn't reach their ends.
All inputs are finite; a program needn't handle non-finite values.
Results may differ from the reference program's by a relative error of at most 0.01.
Values may be sent and summed in bfloat16 or wider, within the bound.
No kernel may reach another device: no remote copies, remote signals or barrier semaphores. Data moves between devices by JAX's collectives and lax.ppermute only.
A program may use at most 64 MiB of HBM per device.

```python
import math
import jax
import jax.numpy as jnp
from jax import lax

D = 1536
CKPT = 8
LATENTS = 8192
BATCH = 640


def block_scale(rng, dims, pieces, low, largest):
    def one(position, shards_of):
        heights = jax.random.uniform(jax.random.fold_in(jax.random.fold_in(rng, 6), position), (shards_of,), jnp.float32, low / len(pieces), largest / len(pieces))
        return jnp.repeat(jnp.exp(heights), dims[position] // shards_of).reshape((-1,) + (1,) * (len(dims) - position - 1))

    level = one(*pieces[0])
    for cut in pieces[1:]:
        level = level * one(*cut)
    return level


def centred(rng, extent, deviation, most, shards=(), dtype=jnp.bfloat16):
    array = jax.random.normal(rng, extent, jnp.float32) * deviation
    if len(shards) > 0:
        array = block_scale(rng, extent, shards, -0.22, 0.18) * array
    return jnp.clip(array, min=-most, max=most).astype(dtype)


def setup_inputs(seed: int = 0) -> dict:
    seeds = jax.random.split(jax.random.key(seed), 8)
    activations = centred(seeds[0], (CKPT, BATCH, D), 1.0, 6.0, ((0, 8), (1, 64)))
    enc_weight = centred(seeds[1], (CKPT, D, LATENTS), (CKPT * D) ** -0.5, 0.0546875, ((0, 8), (2, 64)))
    enc_bias = centred(seeds[2], (LATENTS,), 0.5, 3.0, ((0, 64),), jnp.float32)
    dec_weight = centred(seeds[3], (LATENTS, CKPT, D), (LATENTS // 4) ** -0.5, 0.125, ((0, 64), (1, 8)))
    dec_bias = centred(seeds[4], (CKPT, D), 0.5, 3.0, ((0, 8),), jnp.float32)
    dec_first = centred(seeds[5], (LATENTS, CKPT, D), 0.05, 0.3, ((0, 64), (1, 8)), jnp.float32)
    dec_second = jnp.clip(jnp.exp(math.log(2.0) - 3.6888794 * jax.random.uniform(seeds[6], (LATENTS, CKPT, D), jnp.float32) ** block_scale(seeds[6], (LATENTS, CKPT, D), ((0, 64), (1, 8)), -0.2, 0.2)), 0.05, 2.0)
    return dict(activations=activations, enc_weight=enc_weight, enc_bias=enc_bias, dec_weight=dec_weight, dec_bias=dec_bias, dec_first=dec_first, dec_second=dec_second)


sparsity_weight = 1.0
learn_rate = 0.001
beta_first = 0.9
beta_second = 0.999
corr_first = 0.6513215599
corr_second = 0.0099551198
adam_epsilon = 1e-08
norm_epsilon = 1e-06

def reference(activations, enc_weight, enc_bias, dec_weight, dec_bias, dec_first, dec_second):
    members = activations.shape[0]
    batch_rows = activations.shape[1]
    preact = jnp.zeros((batch_rows, enc_weight.shape[2]), jnp.float32)
    for member in range(members):
        preact = preact + jnp.dot(activations[member], enc_weight[member], preferred_element_type=jnp.float32)
    preact = preact + enc_bias[None, :]
    active = jnp.maximum(preact, 0.0)
    codes = active.astype(jnp.bfloat16)
    code_total = lax.optimization_barrier(jnp.sum(active, axis=0))
    dec_float = dec_weight.astype(jnp.float32)
    dec_norms = jnp.sqrt(lax.optimization_barrier(jnp.sum(dec_float * dec_float, axis=2)) + norm_epsilon)
    norm_total = lax.optimization_barrier(jnp.sum(dec_norms, axis=1))
    scale_rec = 2.0 / batch_rows
    scale_sparse = sparsity_weight / batch_rows
    err_grad = jnp.zeros((batch_rows, enc_weight.shape[2]), jnp.float32)
    dec_terms = []
    for member in range(members):
        decoded = jnp.dot(codes, dec_weight[:, member, :], preferred_element_type=jnp.float32) + dec_bias[member][None, :]
        errors = (decoded - activations[member].astype(jnp.float32)).astype(jnp.bfloat16)
        err_grad = err_grad + jnp.dot(errors, dec_weight[:, member, :].T, preferred_element_type=jnp.float32)
        dec_terms.append(jnp.dot(codes.T, errors, preferred_element_type=jnp.float32))
    dec_term = jnp.stack(dec_terms, axis=1)
    grad_code = scale_rec * err_grad + scale_sparse * norm_total[None, :]
    grad_pre = jnp.where(preact > 0.0, grad_code, 0.0).astype(jnp.bfloat16)
    enc_grad = jnp.stack([jnp.dot(activations[member].T, grad_pre, preferred_element_type=jnp.float32) for member in range(members)], axis=0).astype(jnp.bfloat16)
    dec_grad = scale_rec * dec_term + scale_sparse * code_total[:, None, None] * dec_float / dec_norms[:, :, None]
    new_first = beta_first * dec_first + (1.0 - beta_first) * dec_grad
    new_second = beta_second * dec_second + (1.0 - beta_second) * dec_grad * dec_grad
    new_decoder = dec_float - learn_rate * (new_first / corr_first) / (jnp.sqrt(new_second / corr_second) + adam_epsilon)
    return (enc_grad, new_decoder, new_first, new_second)
```

```python
import jax
import jax.numpy as jnp
from jax import lax
from jax.sharding import PartitionSpec as P

sparsity_weight = 1.0
learn_rate = 0.001
beta_first = 0.9
beta_second = 0.999
corr_first = 0.6513215599
corr_second = 0.0099551198
adam_epsilon = 1e-08
norm_epsilon = 1e-06

CHUNKS = (4, 6)
BOTH = ("snap", "lat")
LANES = 128


def mm(left, right, dims):
    return lax.dot_general(left, right, (dims, ((), ())), preferred_element_type=jnp.float32)


def swap(x, core, own, other):
    low = jnp.where(core == 0, own, other)
    high = jnp.where(core == 0, other, own)
    return jnp.concatenate([low, high], axis=x)


def body(activations, enc_weight, enc_bias, dec_weight, dec_bias, dec_first, dec_second):
    snaps = lax.axis_size("snap")
    lats = lax.axis_size("lat")
    rows_dev, width = activations.shape[1:]
    lat_dev = enc_weight.shape[2]
    half = width // 2
    quarter = half // 2
    batch_rows = rows_dev * lats
    scale_rec = 2.0 / batch_rows
    scale_sparse = sparsity_weight / batch_rows
    snap = lax.axis_index("snap")
    lat = lax.axis_index("lat")
    core = lat % 2
    chip = lat // 2
    pair_groups = [[c * lats + 2 * j + k for c in range(snaps) for k in range(2)] for j in range(lats // 2)]
    chip_groups = [[2 * j + k for j in range(lats // 2)] for k in range(2)]
    partner = [(i, i ^ 1) for i in range(lats)]
    pairs = 2 * snaps
    chips = lats // 2

    def over_pairs(x):
        return lax.all_to_all(x, BOTH, 0, 0, tiled=True, axis_index_groups=pair_groups)

    def over_chips(x):
        return lax.all_to_all(x, "lat", 0, 0, tiled=True, axis_index_groups=chip_groups)

    def exchange(x):
        return lax.ppermute(x, "lat", partner)

    rows = activations[0]
    enc_local = enc_weight[0]
    dec_local = dec_weight[:, 0, :]

    gathered = []
    first = 0
    for size in CHUNKS:
        part = rows[first : first + size].reshape(size, 2, half).transpose(1, 0, 2)
        part = part.reshape(1, 2, size * half // LANES, LANES)
        sent = jnp.broadcast_to(part, (chips,) + part.shape[1:]).reshape((lats,) + part.shape[2:])
        got = lax.all_to_all(sent, "lat", 0, 0, tiled=True)
        gathered.append(got.reshape(lats * size, half))
        first += size

    enc_split = enc_local.reshape(2, half, lat_dev)
    enc_own = lax.dynamic_index_in_dim(enc_split, core, 0, keepdims=False)
    enc_other = exchange(lax.dynamic_index_in_dim(enc_split, 1 - core, 0, keepdims=False))
    enc_pair = swap(1, core, enc_own, enc_other)
    dec_own = lax.dynamic_slice_in_dim(dec_local, core * half, half, 1)
    dec_other = exchange(lax.dynamic_slice_in_dim(dec_local, (1 - core) * half, half, 1))
    dec_pair = swap(0, core, dec_own, dec_other)
    dec_float = dec_local.astype(jnp.float32)
    own_norm = jnp.sqrt(jnp.sum(dec_float * dec_float, axis=1) + norm_epsilon)
    nothing = jnp.zeros_like(own_norm)
    norm_part = scale_sparse * swap(0, core, own_norm, nothing)
    bias_part = jnp.where(snap == 0, swap(0, core, enc_bias, nothing), 0.0)

    place_col = chip // (chips // 2)
    place_row = chip % (chips // 2)
    bias_block = lax.dynamic_slice_in_dim(dec_bias[0], core * half + place_col * quarter, quarter, 0)

    pres = []
    for a in gathered:
        partial = mm(a, enc_pair, ((1,), (0,))) + bias_part[None, :]
        count = a.shape[0] // pairs
        pres.append(jnp.sum(over_pairs(partial.reshape(pairs, count, 2 * lat_dev)), axis=0))

    codes_all = []
    for pre in pres:
        codes_block = jnp.maximum(pre, 0.0).astype(jnp.bfloat16)
        sent = jnp.broadcast_to(codes_block[None], (pairs,) + codes_block.shape)
        codes_all.append(over_pairs(sent).reshape(-1, 2 * lat_dev))

    errors_all = []
    for a, codes in zip(gathered, codes_all):
        count = a.shape[0] // (chips // 2)
        sent = jnp.concatenate(
            [
                mm(codes, dec_pair[:, i * quarter : (i + 1) * quarter], ((1,), (0,)))
                .astype(jnp.bfloat16)
                .reshape(chips // 2, count, quarter)
                for i in range(2)
            ],
            axis=0,
        )
        decoded = jnp.sum(over_chips(sent).astype(jnp.float32), axis=0)
        target = lax.dynamic_slice(a, (place_row * count, place_col * quarter), (count, quarter))
        errors = (decoded + bias_block[None, :] - target.astype(jnp.float32)).astype(jnp.bfloat16)
        got = over_chips(jnp.broadcast_to(errors[None], (chips,) + errors.shape))
        got = got.reshape(2, a.shape[0], quarter)
        errors_all.append(jnp.concatenate([got[0], got[1]], axis=1))

    grads = []
    for errors, pre in zip(errors_all, pres):
        partial = scale_rec * mm(errors, dec_pair, ((1,), (1,))) + norm_part[None, :]
        partial = partial.astype(jnp.bfloat16).reshape((pairs,) + pre.shape)
        grad = jnp.sum(over_pairs(partial).astype(jnp.float32), axis=0)
        grad_block = jnp.where(pre > 0.0, grad, 0.0).astype(jnp.bfloat16)
        sent = grad_block.reshape(pre.shape[0], 2, lat_dev).transpose(1, 0, 2)
        sent = jnp.broadcast_to(sent[None], (snaps,) + sent.shape).reshape((pairs,) + sent.shape[1:])
        grads.append(over_pairs(sent).reshape(-1, lat_dev))

    dec_acc = sum(mm(c, e, ((0,), (0,))) for c, e in zip(codes_all, errors_all))
    dec_acc = dec_acc.reshape(2, lat_dev, half)
    acc_own = lax.dynamic_index_in_dim(dec_acc, core, 0, keepdims=False)
    acc_other = exchange(lax.dynamic_index_in_dim(dec_acc, 1 - core, 0, keepdims=False))
    dec_term = swap(1, core, acc_own, acc_other)
    code_pair = sum(jnp.sum(c.astype(jnp.float32), axis=0) for c in codes_all)
    code_total = lax.dynamic_slice_in_dim(code_pair, core * lat_dev, lat_dev, 0)
    dec_grad = scale_rec * dec_term + scale_sparse * code_total[:, None] * dec_float / own_norm[:, None]
    dec_grad = dec_grad[:, None, :]
    new_first = beta_first * dec_first + (1.0 - beta_first) * dec_grad
    new_second = beta_second * dec_second + (1.0 - beta_second) * dec_grad * dec_grad
    new_decoder = dec_float[:, None, :] - learn_rate * (new_first / corr_first) / (
        jnp.sqrt(new_second / corr_second) + adam_epsilon
    )

    enc_half_own = sum(mm(a, g, ((0,), (0,))) for a, g in zip(gathered, grads))
    enc_half_other = sum(mm(exchange(a), g, ((0,), (0,))) for a, g in zip(gathered, grads))
    enc_grad = swap(0, core, enc_half_own.astype(jnp.bfloat16), enc_half_other.astype(jnp.bfloat16))[None]
    return (enc_grad, new_decoder, new_first, new_second)


def solution(mesh):
    in_specs = (
        P("snap", "lat", None),
        P("snap", None, "lat"),
        P("lat"),
        P("lat", "snap", None),
        P("snap", None),
        P("lat", "snap", None),
        P("lat", "snap", None),
    )
    out_specs = (
        P("snap", None, "lat"),
        P("lat", "snap", None),
        P("lat", "snap", None),
        P("lat", "snap", None),
    )
    return jax.shard_map(body, mesh=mesh, in_specs=in_specs, out_specs=out_specs, check_vma=False)
```

```python
import jax
import jax.numpy as jnp
from jax import lax
from jax.sharding import PartitionSpec as P

sparsity_weight = 1.0
learn_rate = 0.001
beta_first = 0.9
beta_second = 0.999
corr_first = 0.6513215599
corr_second = 0.0099551198
adam_epsilon = 1e-08
norm_epsilon = 1e-06

LANES = 128


def mm(left, right, dims):
    return lax.dot_general(left, right, (dims, ((), ())), preferred_element_type=jnp.float32)


def pick(x, size, index):
    return lax.dynamic_slice_in_dim(x, index * size, size, x.ndim - 1)


def body(activations, enc_weight, enc_bias, dec_weight, dec_bias, dec_first, dec_second):
    snaps = lax.axis_size("snap")
    lats = lax.axis_size("lat")
    rows_dev, width = activations.shape[1:]
    lat_dev = enc_weight.shape[2]
    half = width // 2
    quarter = half // 2
    batch_rows = rows_dev * lats
    block_rows = batch_rows // snaps
    scale_rec = 2.0 / batch_rows
    scale_sparse = sparsity_weight / batch_rows
    lat = lax.axis_index("lat")
    core = lax.bitwise_and(lat, 1)
    chip = lax.shift_right_logical(lat, 1)
    chips = lats // 2
    chip_groups = [[2 * j + k for j in range(chips)] for k in range(2)]
    partner = [(i, i ^ 1) for i in range(lats)]

    def over_snaps(x):
        return lax.all_to_all(x, "snap", 0, 0, tiled=True)

    def over_chips(x):
        return lax.all_to_all(x, "lat", 0, 0, tiled=True, axis_index_groups=chip_groups)

    def exchange(x):
        return lax.ppermute(x, "lat", partner)

    def repeat(x, times):
        return jnp.broadcast_to(x[None], (times,) + x.shape)

    def ordered(axis, own, other):
        low = jnp.where(core == 0, own, other)
        high = jnp.where(core == 0, other, own)
        return jnp.concatenate([low, high], axis=axis)

    rows = activations[0]
    enc_local = enc_weight[0]
    dec_local = dec_weight[:, 0, :]

    part = rows.reshape(rows_dev, 2, half).transpose(1, 0, 2)
    part = part.reshape(2, rows_dev * half // LANES, LANES)
    sent = repeat(part, chips).reshape((lats,) + part.shape[1:])
    acts = lax.all_to_all(sent, "lat", 0, 0, tiled=True).reshape(batch_rows, half)

    enc_split = enc_local.reshape(2, half, lat_dev)
    enc_own = lax.dynamic_index_in_dim(enc_split, core, 0, keepdims=False)
    enc_other = exchange(lax.dynamic_index_in_dim(enc_split, 1 - core, 0, keepdims=False))
    dec_own = pick(dec_local, half, core)
    dec_other = exchange(pick(dec_local, half, 1 - core))
    dec_pair = jnp.concatenate([dec_own, dec_other], axis=0)
    dec_float = dec_local.astype(jnp.float32)
    own_norm = jnp.sqrt(jnp.sum(dec_float * dec_float, axis=1) + norm_epsilon)

    pre_other = exchange(mm(acts, enc_other, ((1,), (0,))))
    pre_own = mm(acts, enc_own, ((1,), (0,)))
    pre = jnp.sum(over_snaps((pre_own + pre_other).reshape(snaps, block_rows, lat_dev)), axis=0) + enc_bias[None, :]

    codes_block = jnp.maximum(pre, 0.0).astype(jnp.bfloat16)
    codes = over_snaps(repeat(codes_block, snaps)).reshape(batch_rows, lat_dev)
    codes_pair = jnp.concatenate([codes, exchange(codes)], axis=1)

    count = batch_rows // (chips // 2)
    place_col = lax.div(chip, chips // 2)
    place_row = lax.rem(chip, chips // 2)
    sent = jnp.stack(
        [
            mm(codes_pair, dec_pair[:, i * quarter : (i + 1) * quarter], ((1,), (0,))).astype(jnp.bfloat16)
            for i in range(2)
        ],
        axis=0,
    ).reshape(chips, count, quarter)
    decoded = jnp.sum(over_chips(sent).astype(jnp.float32), axis=0)
    target = lax.dynamic_slice(acts, (place_row * count, place_col * quarter), (count, quarter))
    bias_block = lax.dynamic_slice_in_dim(dec_bias[0], core * half + place_col * quarter, quarter, 0)
    errors_block = (decoded + bias_block[None, :] - target.astype(jnp.float32)).astype(jnp.bfloat16)
    got = over_chips(repeat(errors_block, chips)).reshape(2, batch_rows, quarter)
    errors = jnp.concatenate([got[0], got[1]], axis=1)

    grad_pair = mm(errors, dec_pair, ((1,), (1,)))
    grad_other = exchange((scale_rec * grad_pair[:, lat_dev:]).astype(jnp.bfloat16))
    grad_own = scale_rec * grad_pair[:, :lat_dev] + grad_other.astype(jnp.float32) + scale_sparse * own_norm[None, :]
    grad_own = grad_own.astype(jnp.bfloat16).reshape(snaps, block_rows, lat_dev)
    grad_own, errors_late = lax.optimization_barrier((grad_own, errors))
    grad = jnp.sum(over_snaps(grad_own).astype(jnp.float32), axis=0)
    grad_block = jnp.where(pre > 0.0, grad, 0.0).astype(jnp.bfloat16)
    grad_pre = over_snaps(repeat(grad_block, snaps)).reshape(batch_rows, lat_dev)

    acc_pair = mm(codes_pair, errors_late, ((0,), (0,)))
    dec_term = ordered(1, acc_pair[:lat_dev], exchange(acc_pair[lat_dev:]))
    code_total = jnp.sum(codes.astype(jnp.float32), axis=0)
    dec_grad = scale_rec * dec_term + scale_sparse * code_total[:, None] * dec_float / own_norm[:, None]
    dec_grad = dec_grad[:, None, :]
    new_first = beta_first * dec_first + (1.0 - beta_first) * dec_grad
    new_second = beta_second * dec_second + (1.0 - beta_second) * dec_grad * dec_grad
    new_decoder = dec_float[:, None, :] - learn_rate * (new_first / corr_first) / (
        jnp.sqrt(new_second / corr_second) + adam_epsilon
    )

    acts_both = lax.optimization_barrier(ordered(0, acts.T, exchange(acts).T))
    enc_grad = mm(acts_both, grad_pre, ((1,), (0,))).astype(jnp.bfloat16)[None]
    return (enc_grad, new_decoder, new_first, new_second)


def solution(mesh):
    in_specs = (
        P("snap", "lat", None),
        P("snap", None, "lat"),
        P("lat"),
        P("lat", "snap", None),
        P("snap", None),
        P("lat", "snap", None),
        P("lat", "snap", None),
    )
    out_specs = (
        P("snap", None, "lat"),
        P("lat", "snap", None),
        P("lat", "snap", None),
        P("lat", "snap", None),
    )
    return jax.shard_map(body, mesh=mesh, in_specs=in_specs, out_specs=out_specs, check_vma=False)
```

```python
import jax
import jax.numpy as jnp
from jax import lax
from jax.experimental import pallas as pl
from jax.experimental.pallas import tpu as pltpu
from jax.sharding import PartitionSpec as P


sparsity_weight = 1.0
learn_rate = 0.001
beta_first = 0.9
beta_second = 0.999
corr_first = 0.6513215599
corr_second = 0.0099551198
adam_epsilon = 1e-08
norm_epsilon = 1e-06

LANES = 128
TEAM = 4


def mm(left, right, dims):
    return lax.dot_general(left, right, (dims, ((), ())), preferred_element_type=jnp.float32)


def encoder_kernel(core_ref, own_ref, other_ref, grad_ref, out_ref):
    grad = grad_ref[...].astype(jnp.float32).T.astype(jnp.bfloat16)
    for mask, half in enumerate((own_ref, other_ref)):
        term = lax.dot_general(grad, half[...], (((1,), (0,)), ((), ())), preferred_element_type=jnp.float32)
        out_ref[core_ref[0] ^ mask] = term.T.astype(jnp.bfloat16)


def encoder_grad(core, own, other, grad):
    half, lat_dev = own.shape[1], grad.shape[1]
    return pl.pallas_call(
        encoder_kernel,
        out_shape=jax.ShapeDtypeStruct((2, half, lat_dev), jnp.bfloat16),
        in_specs=[pl.BlockSpec(memory_space=pltpu.SMEM)] + [pl.BlockSpec(memory_space=pltpu.VMEM)] * 3,
        out_specs=pl.BlockSpec(memory_space=pltpu.VMEM),
        name="encoder_grad",
    )(core, own, other, grad)


def adam_kernel(place_ref, p0, p1, p2, p3, weight_ref, coef_ref, first_ref, second_ref, dec_out, first_out, second_out, term):
    lats, part = p0.shape
    tiles = TEAM * part // LANES
    for mask, piece in enumerate((p0, p1, p2, p3)):
        term[place_ref[0] ^ mask] = piece[...]
    for tile in range(tiles):
        col = tile * LANES % part
        rows = pl.ds(tile, lats, stride=tiles)
        weight = weight_ref[:, tile * LANES : (tile + 1) * LANES].astype(jnp.float32)
        grad = term[tile * LANES // part, :, col : col + LANES] + coef_ref[...] * weight
        first = beta_first * first_ref[rows, :] + (1.0 - beta_first) * grad
        second = beta_second * second_ref[rows, :] + (1.0 - beta_second) * grad * grad
        first_out[rows, :] = first
        second_out[rows, :] = second
        dec_out[rows, :] = weight - learn_rate * (first / corr_first) / (jnp.sqrt(second / corr_second) + adam_epsilon)


def adam(place, pieces, weight, coef, first, second):
    lat_dev, width = weight.shape
    part = width // TEAM
    steps = 4
    lats = lat_dev // steps
    rows = lats * width // LANES
    flat = jax.ShapeDtypeStruct((lat_dev * width // LANES, LANES), jnp.float32)
    by_lat = lambda size: pl.BlockSpec((lats, size), lambda i: (i, 0))
    by_row = pl.BlockSpec((rows, LANES), lambda i: (i, 0))
    outs = pl.pallas_call(
        adam_kernel,
        grid=(steps,),
        out_shape=(flat, flat, flat),
        in_specs=[pl.BlockSpec(memory_space=pltpu.SMEM)]
        + [by_lat(part)] * TEAM
        + [by_lat(width), by_lat(1), by_row, by_row],
        out_specs=(by_row, by_row, by_row),
        scratch_shapes=[pltpu.VMEM((TEAM, lats, part), jnp.float32)],
        name="adam",
    )(place, *pieces, weight, coef, first.reshape(flat.shape), second.reshape(flat.shape))
    return [out.reshape(lat_dev, 1, width) for out in outs]


def body(activations, enc_weight, enc_bias, dec_weight, dec_bias, dec_first, dec_second):
    snaps = lax.axis_size("snap")
    lats = lax.axis_size("lat")
    rows_dev, width = activations.shape[1:]
    lat_dev = enc_weight.shape[2]
    part = width // TEAM
    half = width // 2
    batch_rows = rows_dev * lats
    block_rows = batch_rows // snaps
    teams = lats // TEAM
    team_rows = batch_rows // teams
    scale_rec = 2.0 / batch_rows
    scale_sparse = sparsity_weight / batch_rows
    lat = lax.axis_index("lat")
    team = lax.shift_right_logical(lat, 2)
    core = lax.bitwise_and(lat, 1)
    chip = lax.bitwise_and(lax.shift_right_logical(lat, 1), 1)
    place = 2 * core + chip
    place_groups = [[t * TEAM + p for t in range(teams)] for p in range(TEAM)]
    pair_groups = [
        [c * lats + t * TEAM + 2 * z + k for z in range(2) for c in range(snaps)]
        for t in range(teams)
        for k in range(2)
    ]

    def over_snaps(x):
        return lax.all_to_all(x, "snap", 0, 0, tiled=True)

    def over_pairs(x):
        return lax.all_to_all(x, ("snap", "lat"), 0, 0, tiled=True, axis_index_groups=pair_groups)

    def over_teams(x):
        return lax.all_to_all(x, "lat", 0, 0, tiled=True, axis_index_groups=place_groups)

    def exchange(x, mask):
        return lax.ppermute(x, "lat", [(i, i ^ mask) for i in range(lats)])

    def repeat(x, times):
        return jnp.broadcast_to(x[None], (times,) + x.shape)

    def by_chip(same, other, axis):
        return jnp.concatenate(
            [jnp.where(chip == 0, same, other), jnp.where(chip == 0, other, same)], axis=axis
        )

    def split(x, axis, index):
        size = x.shape[axis] // 2
        return (
            lax.dynamic_slice_in_dim(x, index * size, size, axis),
            lax.dynamic_slice_in_dim(x, (1 - index) * size, size, axis),
        )

    CORE, CHIP = 1, 2
    rows = activations[0]
    enc_local = enc_weight[0]
    dec_local = dec_weight[:, 0, :]

    sent = rows.reshape(rows_dev, 2, half).transpose(1, 0, 2)
    sent = sent.reshape(2, rows_dev * half // LANES, LANES)
    sent = repeat(sent, lats // 2).reshape((lats,) + sent.shape[1:])
    acts = lax.all_to_all(sent, "lat", 0, 0, tiled=True)

    enc_own, give = split(enc_local, 0, core)
    enc_other = exchange(give, CORE)
    acts, enc_own, enc_other = lax.optimization_barrier((acts, enc_own, enc_other))
    acts = acts.reshape(batch_rows, half)

    dec_parts = dec_local.reshape(lat_dev, 2, 2, part)
    keep = lax.dynamic_index_in_dim(dec_parts, chip, 2, keepdims=False).reshape(lat_dev, half)
    give = lax.dynamic_index_in_dim(dec_parts, 1 - chip, 2, keepdims=False).reshape(lat_dev, half)
    dec_chips = lax.optimization_barrier(by_chip(keep, exchange(give, CHIP), 0))
    keep, give = split(dec_chips, 1, core)
    dec_other = exchange(give, CORE)
    dec_team = lax.optimization_barrier(jnp.concatenate([keep, dec_other], axis=0))
    dec_float = dec_local.astype(jnp.float32)
    own_norm = jnp.sqrt(jnp.sum(dec_float * dec_float, axis=1) + norm_epsilon)

    pre_other = exchange(mm(acts, enc_other, ((1,), (0,))), CORE)
    pre_sent = (mm(acts, enc_own, ((1,), (0,))) + pre_other).reshape(snaps, block_rows, lat_dev)
    pre = jnp.sum(over_snaps(pre_sent), axis=0) + enc_bias[None, :]

    codes_block = jnp.maximum(pre, 0.0).astype(jnp.bfloat16)
    codes_chips = over_pairs(repeat(codes_block, 2 * snaps)).reshape(2, batch_rows, lat_dev)
    codes_core = jnp.concatenate([codes_chips[0], codes_chips[1]], axis=1)
    acts_other = exchange(acts, CORE)
    codes = jnp.concatenate([codes_core, exchange(codes_core, CORE)], axis=1)

    sent = mm(codes, dec_team, ((1,), (0,))).astype(jnp.bfloat16).reshape(teams, team_rows, part)
    decoded = jnp.sum(over_teams(sent).astype(jnp.float32), axis=0)
    target = lax.dynamic_slice(acts, (team * team_rows, chip * part), (team_rows, part))
    bias_part = lax.dynamic_slice_in_dim(dec_bias[0], place * part, part, 0)
    errors_block = (decoded + bias_part[None, :] - target.astype(jnp.float32)).astype(jnp.bfloat16)
    errors = over_teams(repeat(errors_block, teams)).reshape(batch_rows, part)

    grad_other = exchange((scale_rec * mm(errors, dec_team[2 * lat_dev :], ((1,), (1,)))).astype(jnp.bfloat16), 1)
    norm_part = scale_sparse * own_norm[None, :]
    grad_sent = jnp.stack(
        [
            scale_rec * mm(errors, dec_team[z * lat_dev : (z + 1) * lat_dev], ((1,), (1,)))
            + grad_other[:, z * lat_dev : (z + 1) * lat_dev].astype(jnp.float32)
            + jnp.where(chip == z, norm_part, 0.0)
            for z in range(2)
        ],
        axis=0,
    ).astype(jnp.bfloat16)
    grad_sent = grad_sent.reshape(2 * snaps, block_rows, lat_dev)
    grad = jnp.sum(over_pairs(grad_sent).astype(jnp.float32), axis=0)
    grad_block = jnp.where(pre > 0.0, grad, 0.0).astype(jnp.bfloat16)
    grad_pre = over_snaps(repeat(grad_block, snaps)).reshape(batch_rows, lat_dev)

    acc_own = scale_rec * mm(codes[:, : 2 * lat_dev], errors, ((0,), (0,)))
    acc_give = scale_rec * mm(codes[:, 2 * lat_dev :], errors, ((0,), (0,)))
    acc_core = exchange(acc_give, CORE)
    keep, give = split(jnp.stack([acc_own, acc_core], axis=0), 1, chip)
    acc_chip = exchange(give, CHIP)
    own_codes = lax.dynamic_index_in_dim(codes_chips, chip, 0, keepdims=False)
    code_total = jnp.sum(own_codes.astype(jnp.float32), axis=0)
    coef = (scale_sparse * code_total / own_norm)[:, None]
    pieces = (keep[0], acc_chip[0], keep[1], acc_chip[1])
    new_decoder, new_first, new_second = adam(place.reshape(1), pieces, dec_local, coef, dec_first, dec_second)

    enc_grad = encoder_grad(core.reshape(1), acts, acts_other, grad_pre).reshape(1, width, lat_dev)
    return (enc_grad, new_decoder, new_first, new_second)


def solution(mesh):
    in_specs = (
        P("snap", "lat", None),
        P("snap", None, "lat"),
        P("lat"),
        P("lat", "snap", None),
        P("snap", None),
        P("lat", "snap", None),
        P("lat", "snap", None),
    )
    out_specs = (
        P("snap", None, "lat"),
        P("lat", "snap", None),
        P("lat", "snap", None),
        P("lat", "snap", None),
    )

    return jax.shard_map(body, mesh=mesh, in_specs=in_specs, out_specs=out_specs, check_vma=False)
```

```python
import jax
import jax.numpy as jnp
from jax import lax
from jax.experimental import pallas as pl
from jax.experimental.pallas import tpu as pltpu
from jax.sharding import PartitionSpec as P


sparsity_weight = 1.0
learn_rate = 0.001
beta_first = 0.9
beta_second = 0.999
corr_first = 0.6513215599
corr_second = 0.0099551198
adam_epsilon = 1e-08
norm_epsilon = 1e-06

LANES = 128
TEAM = 4


def mm(left, right, dims):
    return lax.dot_general(left, right, (dims, ((), ())), preferred_element_type=jnp.float32)


def encoder_kernel(core_ref, own_ref, other_ref, grad_ref, out_ref):
    grad = grad_ref[...].astype(jnp.float32).T.astype(jnp.bfloat16)
    for mask, half in enumerate((own_ref, other_ref)):
        term = lax.dot_general(grad, half[...], (((1,), (0,)), ((), ())), preferred_element_type=jnp.float32)
        out_ref[core_ref[0] ^ mask] = term.T.astype(jnp.bfloat16)


def encoder_grad(core, own, other, grad):
    half, lat_dev = own.shape[1], grad.shape[1]
    return pl.pallas_call(
        encoder_kernel,
        out_shape=jax.ShapeDtypeStruct((2, half, lat_dev), jnp.bfloat16),
        in_specs=[pl.BlockSpec(memory_space=pltpu.SMEM)] + [pl.BlockSpec(memory_space=pltpu.VMEM)] * 3,
        out_specs=pl.BlockSpec(memory_space=pltpu.VMEM),
        compiler_params=pltpu.CompilerParams(vmem_limit_bytes=12 << 20),
        name="encoder_grad",
    )(core, own, other, grad)


def adam_kernel(place_ref, p0, p1, p2, p3, weight_ref, coef_ref, first_ref, second_ref, dec_out, first_out, second_out, term):
    lats, part = p0.shape
    tiles = TEAM * part // LANES
    for mask, piece in enumerate((p0, p1, p2, p3)):
        term[place_ref[0] ^ mask] = piece[...]
    for tile in range(tiles):
        col = tile * LANES % part
        rows = pl.ds(tile, lats, stride=tiles)
        weight = weight_ref[:, tile * LANES : (tile + 1) * LANES].astype(jnp.float32)
        grad = term[tile * LANES // part, :, col : col + LANES] + coef_ref[...] * weight
        first = beta_first * first_ref[rows, :] + (1.0 - beta_first) * grad
        second = beta_second * second_ref[rows, :] + (1.0 - beta_second) * grad * grad
        first_out[rows, :] = first
        second_out[rows, :] = second
        dec_out[rows, :] = weight - learn_rate * (first / corr_first) / (jnp.sqrt(second / corr_second) + adam_epsilon)


def adam(place, pieces, weight, coef, first, second):
    lat_dev, width = weight.shape
    part = width // TEAM
    steps = 4
    lats = lat_dev // steps
    rows = lats * width // LANES
    flat = jax.ShapeDtypeStruct((lat_dev * width // LANES, LANES), jnp.float32)
    by_lat = lambda size: pl.BlockSpec((lats, size), lambda i: (i, 0))
    by_row = pl.BlockSpec((rows, LANES), lambda i: (i, 0))
    outs = pl.pallas_call(
        adam_kernel,
        grid=(steps,),
        out_shape=(flat, flat, flat),
        in_specs=[pl.BlockSpec(memory_space=pltpu.SMEM)]
        + [by_lat(part)] * TEAM
        + [by_lat(width), by_lat(1), by_row, by_row],
        out_specs=(by_row, by_row, by_row),
        scratch_shapes=[pltpu.VMEM((TEAM, lats, part), jnp.float32)],
        compiler_params=pltpu.CompilerParams(vmem_limit_bytes=12 << 20),
        name="adam",
    )(place, *pieces, weight, coef, first.reshape(flat.shape), second.reshape(flat.shape))
    return [out.reshape(lat_dev, 1, width) for out in outs]


def body(activations, enc_weight, enc_bias, dec_weight, dec_bias, dec_first, dec_second):
    snaps = lax.axis_size("snap")
    lats = lax.axis_size("lat")
    rows_dev, width = activations.shape[1:]
    lat_dev = enc_weight.shape[2]
    part = width // TEAM
    half = width // 2
    batch_rows = rows_dev * lats
    block_rows = batch_rows // snaps
    teams = lats // TEAM
    team_rows = batch_rows // teams
    scale_rec = 2.0 / batch_rows
    scale_sparse = sparsity_weight / batch_rows
    lat = lax.axis_index("lat")
    core = lax.bitwise_and(lat, 1)
    chip = lax.bitwise_and(lax.shift_right_logical(lat, 4), 1)
    team = lax.bitwise_and(lax.shift_right_logical(lat, 1), 7) + 8 * lax.shift_right_logical(lat, 5)
    place = 2 * core + chip

    def member(team, chip, core):
        return 32 * (team // 8) + 16 * chip + 2 * (team % 8) + core

    place_groups = [[member(t, z, k) for t in range(teams)] for k in range(2) for z in range(2)]
    pair_groups = [
        [c * lats + member(t, z, k) for z in range(2) for c in range(snaps)]
        for t in range(teams)
        for k in range(2)
    ]

    def over_snaps(x):
        return lax.all_to_all(x, "snap", 0, 0, tiled=True)

    def over_pairs(x):
        return lax.all_to_all(x, ("snap", "lat"), 0, 0, tiled=True, axis_index_groups=pair_groups)

    def over_teams(x):
        return lax.all_to_all(x, "lat", 0, 0, tiled=True, axis_index_groups=place_groups)

    def exchange(x, mask):
        return lax.ppermute(x, "lat", [(i, i ^ mask) for i in range(lats)])

    def repeat(x, times):
        return jnp.broadcast_to(x[None], (times,) + x.shape)

    def by_chip(same, other, axis):
        return jnp.concatenate(
            [jnp.where(chip == 0, same, other), jnp.where(chip == 0, other, same)], axis=axis
        )

    def split(x, axis, index):
        size = x.shape[axis] // 2
        return (
            lax.dynamic_slice_in_dim(x, index * size, size, axis),
            lax.dynamic_slice_in_dim(x, (1 - index) * size, size, axis),
        )

    CORE, CHIP = 1, 16
    rows = activations[0]
    enc_local = enc_weight[0]
    dec_local = dec_weight[:, 0, :]

    sent = rows.reshape(rows_dev, 2, half).transpose(1, 0, 2)
    sent = sent.reshape(2, rows_dev * half // LANES, LANES)
    sent = repeat(sent, lats // 2).reshape((lats,) + sent.shape[1:])
    acts = lax.all_to_all(sent, "lat", 0, 0, tiled=True)

    enc_own, give = split(enc_local, 0, core)
    enc_other = exchange(give, CORE)
    acts, enc_own, enc_other = lax.optimization_barrier((acts, enc_own, enc_other))
    acts = acts.reshape(batch_rows, half)

    dec_parts = dec_local.reshape(lat_dev, 2, 2, part)
    keep = lax.dynamic_index_in_dim(dec_parts, chip, 2, keepdims=False).reshape(lat_dev, half)
    give = lax.dynamic_index_in_dim(dec_parts, 1 - chip, 2, keepdims=False).reshape(lat_dev, half)
    dec_chips = lax.optimization_barrier(by_chip(keep, exchange(give, CHIP), 0))
    keep, give = split(dec_chips, 1, core)
    dec_other = exchange(give, CORE)
    dec_team = lax.optimization_barrier(jnp.concatenate([keep, dec_other], axis=0))
    dec_float = dec_local.astype(jnp.float32)
    own_norm = jnp.sqrt(jnp.sum(dec_float * dec_float, axis=1) + norm_epsilon)

    pre_other = exchange(mm(acts, enc_other, ((1,), (0,))), CORE)
    pre_sent = (mm(acts, enc_own, ((1,), (0,))) + pre_other).reshape(snaps, block_rows, lat_dev)
    pre = jnp.sum(over_snaps(pre_sent), axis=0) + enc_bias[None, :]

    codes_block = jnp.maximum(pre, 0.0).astype(jnp.bfloat16)
    codes_chips = over_pairs(repeat(codes_block, 2 * snaps)).reshape(2, batch_rows, lat_dev)
    codes_core = jnp.concatenate([codes_chips[0], codes_chips[1]], axis=1)
    acts_other = exchange(acts, CORE)
    codes = jnp.concatenate([codes_core, exchange(codes_core, CORE)], axis=1)

    sent = mm(codes, dec_team, ((1,), (0,))).astype(jnp.bfloat16).reshape(teams, team_rows, part)
    decoded = jnp.sum(over_teams(sent).astype(jnp.float32), axis=0)
    target = lax.dynamic_slice(acts, (team * team_rows, chip * part), (team_rows, part))
    bias_part = lax.dynamic_slice_in_dim(dec_bias[0], place * part, part, 0)
    errors_block = (decoded + bias_part[None, :] - target.astype(jnp.float32)).astype(jnp.bfloat16)
    errors = over_teams(repeat(errors_block, teams)).reshape(batch_rows, part)

    grad_other = exchange((scale_rec * mm(errors, dec_team[2 * lat_dev :], ((1,), (1,)))).astype(jnp.bfloat16), 1)
    norm_part = scale_sparse * own_norm[None, :]
    grad_sent = jnp.stack(
        [
            scale_rec * mm(errors, dec_team[z * lat_dev : (z + 1) * lat_dev], ((1,), (1,)))
            + grad_other[:, z * lat_dev : (z + 1) * lat_dev].astype(jnp.float32)
            + jnp.where(chip == z, norm_part, 0.0)
            for z in range(2)
        ],
        axis=0,
    ).astype(jnp.bfloat16)
    grad_sent = grad_sent.reshape(2 * snaps, block_rows, lat_dev)
    grad = jnp.sum(over_pairs(grad_sent).astype(jnp.float32), axis=0)
    grad_block = jnp.where(pre > 0.0, grad, 0.0).astype(jnp.bfloat16)
    grad_pre = over_snaps(repeat(grad_block, snaps)).reshape(batch_rows, lat_dev)

    acc_own = scale_rec * mm(codes[:, : 2 * lat_dev], errors, ((0,), (0,)))
    acc_give = scale_rec * mm(codes[:, 2 * lat_dev :], errors, ((0,), (0,)))
    acc_core = exchange(acc_give, CORE)
    keep, give = split(jnp.stack([acc_own, acc_core], axis=0), 1, chip)
    acc_chip = exchange(give, CHIP)
    own_codes = lax.dynamic_index_in_dim(codes_chips, chip, 0, keepdims=False)
    code_total = jnp.sum(own_codes.astype(jnp.float32), axis=0)
    coef = (scale_sparse * code_total / own_norm)[:, None]
    pieces = (keep[0], acc_chip[0], keep[1], acc_chip[1])
    new_decoder, new_first, new_second = adam(place.reshape(1), pieces, dec_local, coef, dec_first, dec_second)

    enc_grad = encoder_grad(core.reshape(1), acts, acts_other, grad_pre).reshape(1, width, lat_dev)
    return (enc_grad, new_decoder, new_first, new_second)


def solution(mesh):
    in_specs = (
        P("snap", "lat", None),
        P("snap", None, "lat"),
        P("lat"),
        P("lat", "snap", None),
        P("snap", None),
        P("lat", "snap", None),
        P("lat", "snap", None),
    )
    out_specs = (
        P("snap", None, "lat"),
        P("lat", "snap", None),
        P("lat", "snap", None),
        P("lat", "snap", None),
    )

    return jax.shard_map(body, mesh=mesh, in_specs=in_specs, out_specs=out_specs, check_vma=False)
```

```python
import functools

import jax
import jax.numpy as jnp
from jax import lax
from jax.experimental import pallas as pl
from jax.experimental.pallas import tpu as pltpu
from jax.sharding import PartitionSpec as P


sparsity_weight = 1.0
learn_rate = 0.001
beta_first = 0.9
beta_second = 0.999
corr_first = 0.6513215599
corr_second = 0.0099551198
adam_epsilon = 1e-08
norm_epsilon = 1e-06

LANES = 128
TEAM = 4


def mm(left, right, dims):
    return lax.dot_general(left, right, (dims, ((), ())), preferred_element_type=jnp.float32)


def encoder_kernel(core_ref, own_ref, other_ref, grad_ref, out_ref):
    grad = grad_ref[...].astype(jnp.float32).T.astype(jnp.bfloat16)
    for mask, half in enumerate((own_ref, other_ref)):
        term = lax.dot_general(grad, half[...], (((1,), (0,)), ((), ())), preferred_element_type=jnp.float32)
        out_ref[core_ref[0] ^ mask] = term.T.astype(jnp.bfloat16)


def encoder_grad(core, own, other, grad):
    half, lat_dev = own.shape[1], grad.shape[1]
    return pl.pallas_call(
        encoder_kernel,
        out_shape=jax.ShapeDtypeStruct((2, half, lat_dev), jnp.bfloat16),
        in_specs=[pl.BlockSpec(memory_space=pltpu.SMEM)] + [pl.BlockSpec(memory_space=pltpu.VMEM)] * 3,
        out_specs=pl.BlockSpec(memory_space=pltpu.VMEM),
        compiler_params=pltpu.CompilerParams(vmem_limit_bytes=12 << 20),
        name="encoder_grad",
    )(core, own, other, grad)


def small(**more):
    return dict(compiler_params=pltpu.CompilerParams(vmem_limit_bytes=12 << 20), **more)


def whole(count):
    return [pl.BlockSpec(memory_space=pltpu.VMEM)] * count


def decode_kernel(own_ref, other_ref, weight_ref, out_ref):
    codes = jnp.concatenate([own_ref[0], own_ref[1], other_ref[0], other_ref[1]], axis=1)
    out_ref[...] = lax.dot_general(
        codes, weight_ref[...], (((1,), (0,)), ((), ())), preferred_element_type=jnp.float32
    ).astype(jnp.bfloat16)


def decode(own, other, weight):
    rows, part = own.shape[1], weight.shape[1]
    steps = 4
    codes_spec = pl.BlockSpec((2, rows // steps, own.shape[2]), lambda i: (0, i, 0))
    return pl.pallas_call(
        decode_kernel,
        grid=(steps,),
        out_shape=jax.ShapeDtypeStruct((rows, part), jnp.bfloat16),
        in_specs=[codes_spec, codes_spec, pl.BlockSpec(weight.shape, lambda i: (0, 0))],
        out_specs=pl.BlockSpec((rows // steps, part), lambda i: (i, 0)),
        **small(name="decode"),
    )(own, other, weight)


def grad_kernel(scale, chip_ref, errors_ref, weight_ref, norm_ref, own_ref, other_ref):
    lats = own_ref.shape[2]
    for z in range(TEAM):
        rows = weight_ref[z * lats : (z + 1) * lats, :]
        term = scale * lax.dot_general(
            errors_ref[...], rows, (((1,), (1,)), ((), ())), preferred_element_type=jnp.float32
        )
        if z < 2:
            own_ref[z] = term + jnp.where(chip_ref[0] == z, norm_ref[...], 0.0)
        else:
            other_ref[z - 2] = term.astype(jnp.bfloat16)


def grad_parts(scale, chip, errors, weight, norm):
    shape = (2, errors.shape[0], weight.shape[0] // TEAM)
    return pl.pallas_call(
        functools.partial(grad_kernel, scale),
        out_shape=(jax.ShapeDtypeStruct(shape, jnp.float32), jax.ShapeDtypeStruct(shape, jnp.bfloat16)),
        in_specs=[pl.BlockSpec(memory_space=pltpu.SMEM)] + whole(3),
        out_specs=tuple(whole(2)),
        **small(name="grad_parts"),
    )(chip, errors, weight, norm)


def acc_kernel(scale, chip_ref, own_ref, other_ref, errors_ref, keep_ref, give_ref, core_ref):
    for index, ref in ((0, own_ref), (1, own_ref), (0, other_ref), (1, other_ref)):
        codes = ref[chip_ref[0] ^ index].astype(jnp.float32).T.astype(jnp.bfloat16)
        term = scale * lax.dot_general(
            codes, errors_ref[...], (((1,), (0,)), ((), ())), preferred_element_type=jnp.float32
        )
        if ref is own_ref:
            (give_ref if index else keep_ref)[...] = term
        else:
            core_ref[index] = term


def acc_parts(scale, chip, own, other, errors):
    shape = (own.shape[2], errors.shape[1])
    flat = jax.ShapeDtypeStruct(shape, jnp.float32)
    return pl.pallas_call(
        functools.partial(acc_kernel, scale),
        out_shape=(flat, flat, jax.ShapeDtypeStruct((2,) + shape, jnp.float32)),
        in_specs=[pl.BlockSpec(memory_space=pltpu.SMEM)] + whole(3),
        out_specs=tuple(whole(3)),
        **small(name="acc_parts"),
    )(chip, own, other, errors)


def adam_kernel(place_ref, p0, p1, p2, p3, weight_ref, coef_ref, first_ref, second_ref, dec_out, first_out, second_out, term):
    lats, part = p0.shape
    tiles = TEAM * part // LANES
    for mask, piece in enumerate((p0, p1, p2, p3)):
        term[place_ref[0] ^ mask] = piece[...].reshape(lats, part)
    for tile in range(tiles):
        col = tile * LANES % part
        rows = pl.ds(tile, lats, stride=tiles)
        weight = weight_ref[:, tile * LANES : (tile + 1) * LANES].astype(jnp.float32)
        grad = term[tile * LANES // part, :, col : col + LANES] + coef_ref[...] * weight
        first = beta_first * first_ref[rows, :] + (1.0 - beta_first) * grad
        second = beta_second * second_ref[rows, :] + (1.0 - beta_second) * grad * grad
        first_out[rows, :] = first
        second_out[rows, :] = second
        dec_out[rows, :] = weight - learn_rate * (first / corr_first) / (jnp.sqrt(second / corr_second) + adam_epsilon)


def adam(place, pieces, weight, coef, first, second):
    lat_dev, width = weight.shape
    part = width // TEAM
    steps = 4
    lats = lat_dev // steps
    rows = lats * width // LANES
    flat = jax.ShapeDtypeStruct((lat_dev * width // LANES, LANES), jnp.float32)
    by_lat = lambda size: pl.BlockSpec((lats, size), lambda i: (i, 0))
    by_row = pl.BlockSpec((rows, LANES), lambda i: (i, 0))
    outs = pl.pallas_call(
        adam_kernel,
        grid=(steps,),
        out_shape=(flat, flat, flat),
        in_specs=[pl.BlockSpec(memory_space=pltpu.SMEM)]
        + [by_lat(part), by_lat(part), pl.BlockSpec((1, lats, part), lambda i: (0, i, 0)), by_lat(part)]
        + [by_lat(width), by_lat(1), by_row, by_row],
        out_specs=(by_row, by_row, by_row),
        scratch_shapes=[pltpu.VMEM((TEAM, lats, part), jnp.float32)],
        compiler_params=pltpu.CompilerParams(vmem_limit_bytes=12 << 20),
        name="adam",
    )(place, *pieces, weight, coef, first.reshape(flat.shape), second.reshape(flat.shape))
    return [out.reshape(lat_dev, 1, width) for out in outs]


def body(activations, enc_weight, enc_bias, dec_weight, dec_bias, dec_first, dec_second):
    snaps = lax.axis_size("snap")
    lats = lax.axis_size("lat")
    rows_dev, width = activations.shape[1:]
    lat_dev = enc_weight.shape[2]
    part = width // TEAM
    half = width // 2
    batch_rows = rows_dev * lats
    block_rows = batch_rows // snaps
    teams = lats // TEAM
    team_rows = batch_rows // teams
    scale_rec = 2.0 / batch_rows
    scale_sparse = sparsity_weight / batch_rows
    lat = lax.axis_index("lat")
    team = lax.shift_right_logical(lat, 2)
    core = lax.bitwise_and(lat, 1)
    chip = lax.bitwise_and(lax.shift_right_logical(lat, 1), 1)
    place = 2 * core + chip
    place_groups = [[t * TEAM + p for t in range(teams)] for p in range(TEAM)]
    pair_groups = [
        [c * lats + t * TEAM + 2 * z + k for z in range(2) for c in range(snaps)]
        for t in range(teams)
        for k in range(2)
    ]

    def over_snaps(x):
        return lax.all_to_all(x, "snap", 0, 0, tiled=True)

    def over_pairs(x):
        return lax.all_to_all(x, ("snap", "lat"), 0, 0, tiled=True, axis_index_groups=pair_groups)

    def over_teams(x):
        return lax.all_to_all(x, "lat", 0, 0, tiled=True, axis_index_groups=place_groups)

    def exchange(x, mask):
        return lax.ppermute(x, "lat", [(i, i ^ mask) for i in range(lats)])

    def repeat(x, times):
        return jnp.broadcast_to(x[None], (times,) + x.shape)

    def by_chip(same, other, axis):
        return jnp.concatenate(
            [jnp.where(chip == 0, same, other), jnp.where(chip == 0, other, same)], axis=axis
        )

    def split(x, axis, index):
        size = x.shape[axis] // 2
        return (
            lax.dynamic_slice_in_dim(x, index * size, size, axis),
            lax.dynamic_slice_in_dim(x, (1 - index) * size, size, axis),
        )

    CORE, CHIP = 1, 2
    rows = activations[0]
    enc_local = enc_weight[0]
    dec_local = dec_weight[:, 0, :]

    sent = rows.reshape(rows_dev, 2, half).transpose(1, 0, 2)
    sent = sent.reshape(2, rows_dev * half // LANES, LANES)
    sent = repeat(sent, lats // 2).reshape((lats,) + sent.shape[1:])
    acts = lax.all_to_all(sent, "lat", 0, 0, tiled=True)

    enc_own, give = split(enc_local, 0, core)
    enc_other = exchange(give, CORE)
    acts, enc_own, enc_other = lax.optimization_barrier((acts, enc_own, enc_other))
    acts = acts.reshape(batch_rows, half)

    dec_parts = dec_local.reshape(lat_dev, 2, 2, part)
    keep = lax.dynamic_index_in_dim(dec_parts, chip, 2, keepdims=False).reshape(lat_dev, half)
    give = lax.dynamic_index_in_dim(dec_parts, 1 - chip, 2, keepdims=False).reshape(lat_dev, half)
    dec_chips = lax.optimization_barrier(by_chip(keep, exchange(give, CHIP), 0))
    keep, give = split(dec_chips, 1, core)
    dec_other = exchange(give, CORE)
    dec_team = lax.optimization_barrier(jnp.concatenate([keep, dec_other], axis=0))
    dec_float = dec_local.astype(jnp.float32)
    own_norm = jnp.sqrt(jnp.sum(dec_float * dec_float, axis=1) + norm_epsilon)

    pre_other = exchange(mm(acts, enc_other, ((1,), (0,))), CORE)
    pre_sent = (mm(acts, enc_own, ((1,), (0,))) + pre_other).reshape(snaps, block_rows, lat_dev)
    pre = jnp.sum(over_snaps(pre_sent), axis=0) + enc_bias[None, :]

    codes_block = jnp.maximum(pre, 0.0).astype(jnp.bfloat16)
    codes_chips = over_pairs(repeat(codes_block, 2 * snaps)).reshape(2, batch_rows, lat_dev)
    codes_other = exchange(codes_chips, CORE)
    acts_other = exchange(acts, CORE)

    sent = decode(codes_chips, codes_other, dec_team).reshape(teams, team_rows, part)
    decoded = jnp.sum(over_teams(sent).astype(jnp.float32), axis=0)
    target = lax.dynamic_slice(acts, (team * team_rows, chip * part), (team_rows, part))
    bias_part = lax.dynamic_slice_in_dim(dec_bias[0], place * part, part, 0)
    errors_block = (decoded + bias_part[None, :] - target.astype(jnp.float32)).astype(jnp.bfloat16)
    errors = over_teams(repeat(errors_block, teams)).reshape(batch_rows, part)

    grad_own, grad_give = grad_parts(scale_rec, chip.reshape(1), errors, dec_team, scale_sparse * own_norm[None, :])
    grad_sent = (grad_own + exchange(grad_give, CORE).astype(jnp.float32)).astype(jnp.bfloat16)
    grad_sent = grad_sent.reshape(2 * snaps, block_rows, lat_dev)
    grad = jnp.sum(over_pairs(grad_sent).astype(jnp.float32), axis=0)
    grad_block = jnp.where(pre > 0.0, grad, 0.0).astype(jnp.bfloat16)
    grad_pre = over_snaps(repeat(grad_block, snaps)).reshape(batch_rows, lat_dev)

    acc_keep, acc_give, acc_core = acc_parts(scale_rec, chip.reshape(1), codes_chips, codes_other, errors)
    acc_core = exchange(acc_core, CORE)
    acc_chip = exchange(acc_give, CHIP)
    acc_both = exchange(acc_core[1], CHIP)
    own_codes = lax.dynamic_index_in_dim(codes_chips, chip, 0, keepdims=False)
    code_total = jnp.sum(own_codes.astype(jnp.float32), axis=0)
    coef = (scale_sparse * code_total / own_norm)[:, None]
    pieces = (acc_keep, acc_chip, acc_core, acc_both)
    new_decoder, new_first, new_second = adam(place.reshape(1), pieces, dec_local, coef, dec_first, dec_second)

    enc_grad = encoder_grad(core.reshape(1), acts, acts_other, grad_pre).reshape(1, width, lat_dev)
    return (enc_grad, new_decoder, new_first, new_second)


def solution(mesh):
    in_specs = (
        P("snap", "lat", None),
        P("snap", None, "lat"),
        P("lat"),
        P("lat", "snap", None),
        P("snap", None),
        P("lat", "snap", None),
        P("lat", "snap", None),
    )
    out_specs = (
        P("snap", None, "lat"),
        P("lat", "snap", None),
        P("lat", "snap", None),
        P("lat", "snap", None),
    )

    return jax.shard_map(body, mesh=mesh, in_specs=in_specs, out_specs=out_specs, check_vma=False)
```

```python
import functools

import jax
import jax.numpy as jnp
from jax import lax
from jax.experimental import pallas as pl
from jax.experimental.pallas import tpu as pltpu
from jax.sharding import PartitionSpec as P


sparsity_weight = 1.0
learn_rate = 0.001
beta_first = 0.9
beta_second = 0.999
corr_first = 0.6513215599
corr_second = 0.0099551198
adam_epsilon = 1e-08
norm_epsilon = 1e-06

LANES = 128
TEAM = 4


def mm(left, right, dims):
    return lax.dot_general(left, right, (dims, ((), ())), preferred_element_type=jnp.float32)


def encoder_kernel(core_ref, own_ref, other_ref, grad_ref, out_ref):
    grad = grad_ref[...].astype(jnp.float32).T.astype(jnp.bfloat16)
    for mask, half in enumerate((own_ref, other_ref)):
        term = lax.dot_general(grad, half[...], (((1,), (0,)), ((), ())), preferred_element_type=jnp.float32)
        out_ref[core_ref[0] ^ mask] = term.T.astype(jnp.bfloat16)


def encoder_grad(core, own, other, grad):
    half, lat_dev = own.shape[1], grad.shape[1]
    return pl.pallas_call(
        encoder_kernel,
        out_shape=jax.ShapeDtypeStruct((2, half, lat_dev), jnp.bfloat16),
        in_specs=[pl.BlockSpec(memory_space=pltpu.SMEM)] + [pl.BlockSpec(memory_space=pltpu.VMEM)] * 3,
        out_specs=pl.BlockSpec(memory_space=pltpu.VMEM),
        compiler_params=pltpu.CompilerParams(vmem_limit_bytes=12 << 20),
        name="encoder_grad",
    )(core, own, other, grad)


def small(**more):
    return dict(compiler_params=pltpu.CompilerParams(vmem_limit_bytes=12 << 20), **more)


def whole(count):
    return [pl.BlockSpec(memory_space=pltpu.VMEM)] * count


def grad_kernel(scale, chip_ref, errors_ref, weight_ref, norm_ref, own_ref, other_ref):
    lats = own_ref.shape[2]
    for z in range(TEAM):
        rows = weight_ref[z * lats : (z + 1) * lats, :]
        term = scale * lax.dot_general(
            errors_ref[...], rows, (((1,), (1,)), ((), ())), preferred_element_type=jnp.float32
        )
        if z < 2:
            own_ref[z] = term + jnp.where(chip_ref[0] == z, norm_ref[...], 0.0)
        else:
            other_ref[z - 2] = term.astype(jnp.bfloat16)


def grad_parts(scale, chip, errors, weight, norm):
    shape = (2, errors.shape[0], weight.shape[0] // TEAM)
    return pl.pallas_call(
        functools.partial(grad_kernel, scale),
        out_shape=(jax.ShapeDtypeStruct(shape, jnp.float32), jax.ShapeDtypeStruct(shape, jnp.bfloat16)),
        in_specs=[pl.BlockSpec(memory_space=pltpu.SMEM)] + whole(3),
        out_specs=tuple(whole(2)),
        **small(name="grad_parts"),
    )(chip, errors, weight, norm)


def acc_kernel(scale, chip_ref, own_ref, other_ref, errors_ref, keep_ref, give_ref, core_ref):
    for index, ref in ((0, own_ref), (1, own_ref), (0, other_ref), (1, other_ref)):
        codes = ref[chip_ref[0] ^ index].astype(jnp.float32).T.astype(jnp.bfloat16)
        term = scale * lax.dot_general(
            codes, errors_ref[...], (((1,), (0,)), ((), ())), preferred_element_type=jnp.float32
        )
        if ref is own_ref:
            (give_ref if index else keep_ref)[...] = term
        else:
            core_ref[index] = term


def acc_parts(scale, chip, own, other, errors):
    shape = (own.shape[2], errors.shape[1])
    flat = jax.ShapeDtypeStruct(shape, jnp.float32)
    return pl.pallas_call(
        functools.partial(acc_kernel, scale),
        out_shape=(flat, flat, jax.ShapeDtypeStruct((2,) + shape, jnp.float32)),
        in_specs=[pl.BlockSpec(memory_space=pltpu.SMEM)] + whole(3),
        out_specs=tuple(whole(3)),
        **small(name="acc_parts"),
    )(chip, own, other, errors)


def adam_kernel(place_ref, p0, p1, p2, p3, weight_ref, coef_ref, first_ref, second_ref, dec_out, first_out, second_out, term):
    lats, part = p0.shape
    tiles = TEAM * part // LANES
    for mask, piece in enumerate((p0, p1, p2, p3)):
        term[place_ref[0] ^ mask] = piece[...].reshape(lats, part)
    for tile in range(tiles):
        col = tile * LANES % part
        rows = pl.ds(tile, lats, stride=tiles)
        weight = weight_ref[:, tile * LANES : (tile + 1) * LANES].astype(jnp.float32)
        grad = term[tile * LANES // part, :, col : col + LANES] + coef_ref[...] * weight
        first = beta_first * first_ref[rows, :] + (1.0 - beta_first) * grad
        second = beta_second * second_ref[rows, :] + (1.0 - beta_second) * grad * grad
        first_out[rows, :] = first
        second_out[rows, :] = second
        dec_out[rows, :] = weight - learn_rate * (first / corr_first) / (jnp.sqrt(second / corr_second) + adam_epsilon)


def adam(place, pieces, weight, coef, first, second):
    lat_dev, width = weight.shape
    part = width // TEAM
    steps = 4
    lats = lat_dev // steps
    rows = lats * width // LANES
    flat = jax.ShapeDtypeStruct((lat_dev * width // LANES, LANES), jnp.float32)
    by_lat = lambda size: pl.BlockSpec((lats, size), lambda i: (i, 0))
    by_row = pl.BlockSpec((rows, LANES), lambda i: (i, 0))
    first_of = pl.BlockSpec((1, lats, part), lambda i: (0, i, 0))
    second_of = pl.BlockSpec((1, lats, part), lambda i: (1, i, 0))
    outs = pl.pallas_call(
        adam_kernel,
        grid=(steps,),
        out_shape=(flat, flat, flat),
        in_specs=[pl.BlockSpec(memory_space=pltpu.SMEM)]
        + [by_lat(part), first_of, first_of, second_of]
        + [by_lat(width), by_lat(1), by_row, by_row],
        out_specs=(by_row, by_row, by_row),
        scratch_shapes=[pltpu.VMEM((TEAM, lats, part), jnp.float32)],
        compiler_params=pltpu.CompilerParams(vmem_limit_bytes=12 << 20),
        name="adam",
    )(place, *pieces, weight, coef, first.reshape(flat.shape), second.reshape(flat.shape))
    return [out.reshape(lat_dev, 1, width) for out in outs]


def body(activations, enc_weight, enc_bias, dec_weight, dec_bias, dec_first, dec_second):
    snaps = lax.axis_size("snap")
    lats = lax.axis_size("lat")
    rows_dev, width = activations.shape[1:]
    lat_dev = enc_weight.shape[2]
    part = width // TEAM
    half = width // 2
    batch_rows = rows_dev * lats
    block_rows = batch_rows // snaps
    teams = lats // TEAM
    team_rows = batch_rows // teams
    scale_rec = 2.0 / batch_rows
    scale_sparse = sparsity_weight / batch_rows
    lat = lax.axis_index("lat")
    team = lax.shift_right_logical(lat, 2)
    core = lax.bitwise_and(lat, 1)
    chip = lax.bitwise_and(lax.shift_right_logical(lat, 1), 1)
    place = 2 * core + chip
    place_groups = [[t * TEAM + p for t in range(teams)] for p in range(TEAM)]
    pair_groups = [
        [c * lats + t * TEAM + 2 * z + k for z in range(2) for c in range(snaps)]
        for t in range(teams)
        for k in range(2)
    ]

    def over_snaps(x):
        return lax.all_to_all(x, "snap", 0, 0, tiled=True)

    def over_pairs(x):
        return lax.all_to_all(x, ("snap", "lat"), 0, 0, tiled=True, axis_index_groups=pair_groups)

    def over_teams(x):
        return lax.all_to_all(x, "lat", 0, 0, tiled=True, axis_index_groups=place_groups)

    def exchange(x, mask):
        return lax.ppermute(x, "lat", [(i, i ^ mask) for i in range(lats)])

    def repeat(x, times):
        return jnp.broadcast_to(x[None], (times,) + x.shape)

    def by_chip(same, other, axis):
        return jnp.concatenate(
            [jnp.where(chip == 0, same, other), jnp.where(chip == 0, other, same)], axis=axis
        )

    def split(x, axis, index):
        size = x.shape[axis] // 2
        return (
            lax.dynamic_slice_in_dim(x, index * size, size, axis),
            lax.dynamic_slice_in_dim(x, (1 - index) * size, size, axis),
        )

    CORE, CHIP = 1, 2
    rows = activations[0]
    enc_local = enc_weight[0]
    dec_local = dec_weight[:, 0, :]

    sent = rows.reshape(rows_dev, 2, half).transpose(1, 0, 2)
    sent = sent.reshape(2, rows_dev * half // LANES, LANES)
    sent = repeat(sent, lats // 2).reshape((lats,) + sent.shape[1:])
    acts = lax.all_to_all(sent, "lat", 0, 0, tiled=True)

    enc_own, give = split(enc_local, 0, core)
    enc_other = exchange(give, CORE)
    acts, enc_own, enc_other = lax.optimization_barrier((acts, enc_own, enc_other))
    acts = acts.reshape(batch_rows, half)

    def chip_parts(index):
        return jnp.concatenate(
            [lax.dynamic_slice_in_dim(dec_local, k * half + index * part, part, 1) for k in range(2)], axis=1
        )

    keep, give = chip_parts(chip), chip_parts(1 - chip)
    dec_chips = lax.optimization_barrier(by_chip(keep, exchange(give, CHIP), 0))
    keep, give = split(dec_chips, 1, core)
    dec_other = exchange(give, CORE)
    dec_team = lax.optimization_barrier(jnp.concatenate([keep, dec_other], axis=0))
    dec_float = dec_local.astype(jnp.float32)
    own_norm = jnp.sqrt(jnp.sum(dec_float * dec_float, axis=1) + norm_epsilon)

    pre_other = exchange(mm(acts, enc_other, ((1,), (0,))), CORE)
    pre_own = lax.optimization_barrier(mm(acts, enc_own, ((1,), (0,))))
    pre_sent = (pre_own + pre_other).reshape(snaps, block_rows, lat_dev)
    pre = jnp.sum(over_snaps(pre_sent), axis=0) + enc_bias[None, :]

    codes_block = jnp.maximum(pre, 0.0).astype(jnp.bfloat16)
    codes_chips = over_pairs(repeat(codes_block, 2 * snaps)).reshape(2, batch_rows, lat_dev)
    codes_other = exchange(codes_chips, CORE)
    acts_other = exchange(acts, CORE)

    codes = jnp.concatenate([codes_chips[0], codes_chips[1], codes_other[0], codes_other[1]], axis=1)
    sent = mm(codes, dec_team, ((1,), (0,))).astype(jnp.bfloat16).reshape(teams, team_rows, part)
    decoded = jnp.sum(over_teams(sent).astype(jnp.float32), axis=0)
    target = lax.dynamic_slice(acts, (team * team_rows, chip * part), (team_rows, part))
    bias_part = lax.dynamic_slice_in_dim(dec_bias[0], place * part, part, 0)
    errors_block = (decoded + bias_part[None, :] - target.astype(jnp.float32)).astype(jnp.bfloat16)
    errors = over_teams(repeat(errors_block, teams)).reshape(batch_rows, part)

    grad_own, grad_give = grad_parts(scale_rec, chip.reshape(1), errors, dec_team, scale_sparse * own_norm[None, :])
    grad_sent = (grad_own + exchange(grad_give, CORE).astype(jnp.float32)).astype(jnp.bfloat16)
    grad_sent = grad_sent.reshape(2 * snaps, block_rows, lat_dev)
    grad = jnp.sum(over_pairs(grad_sent).astype(jnp.float32), axis=0)
    grad_block = jnp.where(pre > 0.0, grad, 0.0).astype(jnp.bfloat16)
    grad_pre = over_snaps(repeat(grad_block, snaps)).reshape(batch_rows, lat_dev)

    acc_keep, acc_give, acc_core = acc_parts(scale_rec, chip.reshape(1), codes_chips, codes_other, errors)
    acc_core = exchange(acc_core, CORE)
    acc_give = lax.optimization_barrier(jnp.stack([acc_give, acc_core[1]], axis=0))
    acc_chip = exchange(acc_give, CHIP)
    own_codes = lax.dynamic_index_in_dim(codes_chips, chip, 0, keepdims=False)
    code_total = jnp.sum(own_codes.astype(jnp.float32), axis=0)
    coef = (scale_sparse * code_total / own_norm)[:, None]
    pieces = (acc_keep, acc_chip, acc_core, acc_chip)
    new_decoder, new_first, new_second = adam(place.reshape(1), pieces, dec_local, coef, dec_first, dec_second)

    enc_grad = encoder_grad(core.reshape(1), acts, acts_other, grad_pre).reshape(1, width, lat_dev)
    return (enc_grad, new_decoder, new_first, new_second)


def solution(mesh):
    in_specs = (
        P("snap", "lat", None),
        P("snap", None, "lat"),
        P("lat"),
        P("lat", "snap", None),
        P("snap", None),
        P("lat", "snap", None),
        P("lat", "snap", None),
    )
    out_specs = (
        P("snap", None, "lat"),
        P("lat", "snap", None),
        P("lat", "snap", None),
        P("lat", "snap", None),
    )

    return jax.shard_map(body, mesh=mesh, in_specs=in_specs, out_specs=out_specs, check_vma=False)
```

```python
import functools

import jax
import jax.numpy as jnp
from jax import lax
from jax.experimental import pallas as pl
from jax.experimental.pallas import tpu as pltpu
from jax.sharding import PartitionSpec as P


sparsity_weight = 1.0
learn_rate = 0.001
beta_first = 0.9
beta_second = 0.999
corr_first = 0.6513215599
corr_second = 0.0099551198
adam_epsilon = 1e-08
norm_epsilon = 1e-06

LANES = 128
TEAM = 4


def mm(left, right, dims):
    return lax.dot_general(left, right, (dims, ((), ())), preferred_element_type=jnp.float32)


def encoder_kernel(core_ref, own_ref, other_ref, grad_ref, out_ref):
    grad = grad_ref[...].astype(jnp.float32).T.astype(jnp.bfloat16)
    for mask, half in enumerate((own_ref, other_ref)):
        term = lax.dot_general(grad, half[...], (((1,), (0,)), ((), ())), preferred_element_type=jnp.float32)
        out_ref[core_ref[0] ^ mask] = term.T.astype(jnp.bfloat16)


def encoder_grad(core, own, other, grad):
    half, lat_dev = own.shape[1], grad.shape[1]
    return pl.pallas_call(
        encoder_kernel,
        out_shape=jax.ShapeDtypeStruct((2, half, lat_dev), jnp.bfloat16),
        in_specs=[pl.BlockSpec(memory_space=pltpu.SMEM)] + [pl.BlockSpec(memory_space=pltpu.VMEM)] * 3,
        out_specs=pl.BlockSpec(memory_space=pltpu.VMEM),
        compiler_params=pltpu.CompilerParams(vmem_limit_bytes=12 << 20),
        name="encoder_grad",
    )(core, own, other, grad)


def small(**more):
    return dict(compiler_params=pltpu.CompilerParams(vmem_limit_bytes=12 << 20), **more)


def whole(count):
    return [pl.BlockSpec(memory_space=pltpu.VMEM)] * count


def grad_kernel(scale, chip_ref, errors_ref, weight_ref, norm_ref, own_ref, other_ref):
    lats = own_ref.shape[2]
    for z in range(TEAM):
        rows = weight_ref[z * lats : (z + 1) * lats, :]
        term = scale * lax.dot_general(
            errors_ref[...], rows, (((1,), (1,)), ((), ())), preferred_element_type=jnp.float32
        )
        if z < 2:
            own_ref[z] = term + jnp.where(chip_ref[0] == z, norm_ref[...], 0.0)
        else:
            other_ref[z - 2] = term.astype(jnp.bfloat16)


def grad_parts(scale, chip, errors, weight, norm):
    shape = (2, errors.shape[0], weight.shape[0] // TEAM)
    return pl.pallas_call(
        functools.partial(grad_kernel, scale),
        out_shape=(jax.ShapeDtypeStruct(shape, jnp.float32), jax.ShapeDtypeStruct(shape, jnp.bfloat16)),
        in_specs=[pl.BlockSpec(memory_space=pltpu.SMEM)] + whole(3),
        out_specs=tuple(whole(2)),
        **small(name="grad_parts"),
    )(chip, errors, weight, norm)


def acc_kernel(scale, chip_ref, own_ref, other_ref, errors_ref, keep_ref, give_ref, core_ref):
    for index, ref in ((0, own_ref), (1, own_ref), (0, other_ref), (1, other_ref)):
        codes = ref[chip_ref[0] ^ index].astype(jnp.float32).T.astype(jnp.bfloat16)
        term = scale * lax.dot_general(
            codes, errors_ref[...], (((1,), (0,)), ((), ())), preferred_element_type=jnp.float32
        )
        if ref is own_ref:
            (give_ref if index else keep_ref)[...] = term
        else:
            core_ref[index] = term


def acc_parts(scale, chip, own, other, errors):
    shape = (own.shape[2], errors.shape[1])
    flat = jax.ShapeDtypeStruct(shape, jnp.float32)
    return pl.pallas_call(
        functools.partial(acc_kernel, scale),
        out_shape=(flat, flat, jax.ShapeDtypeStruct((2,) + shape, jnp.float32)),
        in_specs=[pl.BlockSpec(memory_space=pltpu.SMEM)] + whole(3),
        out_specs=tuple(whole(3)),
        **small(name="acc_parts"),
    )(chip, own, other, errors)


def adam_kernel(place_ref, p0, p1, p2, p3, weight_ref, coef_ref, first_ref, second_ref, dec_out, first_out, second_out, term):
    lats, part = p0.shape
    tiles = TEAM * part // LANES
    for mask, piece in enumerate((p0, p1, p2, p3)):
        term[place_ref[0] ^ mask] = piece[...].reshape(lats, part)
    for tile in range(tiles):
        col = tile * LANES % part
        rows = pl.ds(tile, lats, stride=tiles)
        weight = weight_ref[:, tile * LANES : (tile + 1) * LANES].astype(jnp.float32)
        grad = term[tile * LANES // part, :, col : col + LANES] + coef_ref[...] * weight
        first = beta_first * first_ref[rows, :] + (1.0 - beta_first) * grad
        second = beta_second * second_ref[rows, :] + (1.0 - beta_second) * grad * grad
        first_out[rows, :] = first
        second_out[rows, :] = second
        dec_out[rows, :] = weight - learn_rate * (first / corr_first) / (jnp.sqrt(second / corr_second) + adam_epsilon)


def adam(place, pieces, weight, coef, first, second):
    lat_dev, width = weight.shape
    part = width // TEAM
    steps = 4
    lats = lat_dev // steps
    rows = lats * width // LANES
    flat = jax.ShapeDtypeStruct((lat_dev * width // LANES, LANES), jnp.float32)
    by_lat = lambda size: pl.BlockSpec((lats, size), lambda i: (i, 0))
    by_row = pl.BlockSpec((rows, LANES), lambda i: (i, 0))
    first_of = pl.BlockSpec((1, lats, part), lambda i: (0, i, 0))
    second_of = pl.BlockSpec((1, lats, part), lambda i: (1, i, 0))
    outs = pl.pallas_call(
        adam_kernel,
        grid=(steps,),
        out_shape=(flat, flat, flat),
        in_specs=[pl.BlockSpec(memory_space=pltpu.SMEM)]
        + [by_lat(part), first_of, first_of, second_of]
        + [by_lat(width), by_lat(1), by_row, by_row],
        out_specs=(by_row, by_row, by_row),
        scratch_shapes=[pltpu.VMEM((TEAM, lats, part), jnp.float32)],
        compiler_params=pltpu.CompilerParams(vmem_limit_bytes=12 << 20),
        name="adam",
    )(place, *pieces, weight, coef, first.reshape(flat.shape), second.reshape(flat.shape))
    return [out.reshape(lat_dev, 1, width) for out in outs]


def body(activations, enc_weight, enc_bias, dec_weight, dec_bias, dec_first, dec_second):
    snaps = lax.axis_size("snap")
    lats = lax.axis_size("lat")
    rows_dev, width = activations.shape[1:]
    lat_dev = enc_weight.shape[2]
    part = width // TEAM
    half = width // 2
    batch_rows = rows_dev * lats
    block_rows = batch_rows // snaps
    teams = lats // TEAM
    team_rows = batch_rows // teams
    scale_rec = 2.0 / batch_rows
    scale_sparse = sparsity_weight / batch_rows
    lat = lax.axis_index("lat")
    team = lax.shift_right_logical(lat, 2)
    core = lax.bitwise_and(lat, 1)
    chip = lax.bitwise_and(lax.shift_right_logical(lat, 1), 1)
    place = 2 * core + chip
    place_groups = [[t * TEAM + p for t in range(teams)] for p in range(TEAM)]
    snap_order = [h * (snaps // 2) + x for x in range(snaps // 2) for h in range(2)]
    pair_groups = [
        [c * lats + t * TEAM + 2 * z + k for z in range(2) for c in snap_order]
        for t in range(teams)
        for k in range(2)
    ]

    def over_snaps(x):
        return lax.all_to_all(x, "snap", 0, 0, tiled=True, axis_index_groups=[snap_order])

    def over_pairs(x):
        return lax.all_to_all(x, ("snap", "lat"), 0, 0, tiled=True, axis_index_groups=pair_groups)

    def over_teams(x):
        return lax.all_to_all(x, "lat", 0, 0, tiled=True, axis_index_groups=place_groups)

    def exchange(x, mask):
        return lax.ppermute(x, "lat", [(i, i ^ mask) for i in range(lats)])

    def repeat(x, times):
        return jnp.broadcast_to(x[None], (times,) + x.shape)

    def by_chip(same, other, axis):
        return jnp.concatenate(
            [jnp.where(chip == 0, same, other), jnp.where(chip == 0, other, same)], axis=axis
        )

    def split(x, axis, index):
        size = x.shape[axis] // 2
        return (
            lax.dynamic_slice_in_dim(x, index * size, size, axis),
            lax.dynamic_slice_in_dim(x, (1 - index) * size, size, axis),
        )

    CORE, CHIP = 1, 2
    rows = activations[0]
    enc_local = enc_weight[0]
    dec_local = dec_weight[:, 0, :]

    sent = jnp.stack([rows[:, k * half : (k + 1) * half].reshape(rows_dev * half // LANES, LANES) for k in range(2)])
    sent = repeat(sent, lats // 2).reshape((lats,) + sent.shape[1:])
    acts = lax.all_to_all(sent, "lat", 0, 0, tiled=True)

    enc_own, give = split(enc_local, 0, core)
    enc_other = exchange(give, CORE)
    acts, enc_own, enc_other = lax.optimization_barrier((acts, enc_own, enc_other))
    acts = acts.reshape(batch_rows, half)

    def chip_parts(index):
        return jnp.concatenate(
            [lax.dynamic_slice_in_dim(dec_local, k * half + index * part, part, 1) for k in range(2)], axis=1
        )

    keep, give = chip_parts(chip), chip_parts(1 - chip)
    dec_chips = lax.optimization_barrier(by_chip(keep, exchange(give, CHIP), 0))
    keep, give = split(dec_chips, 1, core)
    dec_other = exchange(give, CORE)
    dec_team = lax.optimization_barrier(jnp.concatenate([keep, dec_other], axis=0))
    dec_float = dec_local.astype(jnp.float32)
    own_norm = jnp.sqrt(jnp.sum(dec_float * dec_float, axis=1) + norm_epsilon)

    pre_other = exchange(mm(acts, enc_other, ((1,), (0,))), CORE)
    pre_own = lax.optimization_barrier(mm(acts, enc_own, ((1,), (0,))))
    pre_sent = (pre_own + pre_other).reshape(snaps, block_rows, lat_dev)
    pre = jnp.sum(over_snaps(pre_sent), axis=0) + enc_bias[None, :]

    codes_block = jnp.maximum(pre, 0.0).astype(jnp.bfloat16)
    codes_chips = over_pairs(repeat(codes_block, 2 * snaps)).reshape(2, batch_rows, lat_dev)
    codes_other = exchange(codes_chips, CORE)
    acts_other = exchange(acts, CORE)

    codes = jnp.concatenate([codes_chips[0], codes_chips[1], codes_other[0], codes_other[1]], axis=1)
    sent = mm(codes, dec_team, ((1,), (0,))).astype(jnp.bfloat16).reshape(teams, team_rows, part)
    decoded = jnp.sum(over_teams(sent).astype(jnp.float32), axis=0)
    target = lax.dynamic_slice(acts, (team * team_rows, chip * part), (team_rows, part))
    bias_part = lax.dynamic_slice_in_dim(dec_bias[0], place * part, part, 0)
    errors_block = (decoded + bias_part[None, :] - target.astype(jnp.float32)).astype(jnp.bfloat16)
    errors = over_teams(repeat(errors_block, teams)).reshape(batch_rows, part)

    grad_own, grad_give = grad_parts(scale_rec, chip.reshape(1), errors, dec_team, scale_sparse * own_norm[None, :])
    grad_sent = (grad_own + exchange(grad_give, CORE).astype(jnp.float32)).astype(jnp.bfloat16)
    grad_sent = grad_sent.reshape(2 * snaps, block_rows, lat_dev)
    grad = jnp.sum(over_pairs(grad_sent).astype(jnp.float32), axis=0)
    grad_block = jnp.where(pre > 0.0, grad, 0.0).astype(jnp.bfloat16)
    grad_pre = over_snaps(repeat(grad_block, snaps)).reshape(batch_rows, lat_dev)

    acc_keep, acc_give, acc_core = acc_parts(scale_rec, chip.reshape(1), codes_chips, codes_other, errors)
    acc_core = exchange(acc_core, CORE)
    acc_give = lax.optimization_barrier(jnp.stack([acc_give, acc_core[1]], axis=0))
    acc_chip = exchange(acc_give, CHIP)
    own_codes = lax.dynamic_index_in_dim(codes_chips, chip, 0, keepdims=False)
    code_total = jnp.sum(own_codes.astype(jnp.float32), axis=0)
    coef = (scale_sparse * code_total / own_norm)[:, None]
    pieces = (acc_keep, acc_chip, acc_core, acc_chip)
    new_decoder, new_first, new_second = adam(place.reshape(1), pieces, dec_local, coef, dec_first, dec_second)

    enc_grad = encoder_grad(core.reshape(1), acts, acts_other, grad_pre).reshape(1, width, lat_dev)
    return (enc_grad, new_decoder, new_first, new_second)


def solution(mesh):
    in_specs = (
        P("snap", "lat", None),
        P("snap", None, "lat"),
        P("lat"),
        P("lat", "snap", None),
        P("snap", None),
        P("lat", "snap", None),
        P("lat", "snap", None),
    )
    out_specs = (
        P("snap", None, "lat"),
        P("lat", "snap", None),
        P("lat", "snap", None),
        P("lat", "snap", None),
    )

    return jax.shard_map(body, mesh=mesh, in_specs=in_specs, out_specs=out_specs, check_vma=False)
```
